32 devices in a mesh: groups: 2 (over x), col: 16 (over z, y, core).
Axes of the slice: x: 2, y: 2, z: 4, core: 2. Of those that a mesh axis runs over, the one named last changes fastest.
Arguments:
- left: bfloat16 [256, 64, 32], P('col', 'groups'), parts along dimension 1, may hold values from -18 to 18
- right: bfloat16 [256, 2560, 32], P('col', 'groups'), parts along dimension 1, may hold values from -18 to 18
- out_weight: bfloat16 [1024, 128], replicated, may hold values from -0.1875 to 0.1875
- out_bias: float32 [128], replicated, may hold values from -3 to 3
Outputs:
- pair_update: bfloat16 [64, 1280, 128], P('groups', 'col'), parts along dimension 0
The draws below stay inside these ranges and needn't reach their ends.
There are 2 independent parts, one for each index of `groups`. The reference program is written for one: setup_inputs(seed, part) draws one part's arguments, and reference() takes and returns one part's arrays. A program takes and returns all parts, laid end to end along the dimension named above; an argument that names none is the same for every part. Nothing has to cross between parts.
All inputs are finite; a program needn't handle non-finite values.
Results may differ from the reference program's by a relative error of at most 0.004.
Values may be sent and summed in bfloat16 or wider, within the bound.
No kernel may reach another device: no remote copies, remote signals or barrier semaphores. Data moves between devices by JAX's collectives and lax.ppermute only.
A program may use at most 64 MiB of HBM per device.

```python
import jax
import jax.numpy as jnp
from jax import lax

C = 32
PAIR = 128
S = 256
COL_DEV = 80
R = 1280
ROWS = 32
CC = 1024
N_COL = 16


def levels(own_key, dims, split, low, largest):
    def one(dim, shards_of):
        heights = jax.random.uniform(jax.random.fold_in(jax.random.fold_in(own_key, 6), dim), (shards_of,), jnp.float32, low / len(split), largest / len(split))
        return jnp.repeat(jnp.exp(heights), dims[dim] // shards_of).reshape((-1,) + (1,) * (len(dims) - dim - 1))

    loudness = one(*split[0])
    for cut in split[1:]:
        loudness = loudness * one(*cut)
    return loudness


def bell_draw(rng, shape, deviation, limit, split=(), kind=jnp.bfloat16):
    level = levels(rng, shape, split, -0.22, 0.18) if split else 1.0
    result = jax.random.normal(rng, shape, jnp.float32) * deviation * level
    return jnp.minimum(jnp.maximum(result, -limit), limit).astype(kind)


def setup_inputs(seed: int = 0, part: int = 0) -> dict:
    key_list = jax.random.split(jax.random.key(seed), 5)
    part_keys = jax.random.split(jax.random.fold_in(key_list[4], part), 5)
    left = bell_draw(part_keys[0], (S, ROWS, C), 3.0, 18.0, ((0, 16),))
    right = bell_draw(part_keys[1], (S, R, C), 3.0, 18.0, ((0, 16),))
    out_weight = bell_draw(key_list[2], (CC, PAIR), CC ** -0.5, 0.1875)
    out_bias = bell_draw(key_list[3], (PAIR,), 0.5, 3.0, (), jnp.float32)
    return {"left": left, "right": right, "out_weight": out_weight, "out_bias": out_bias}


def reference(left, right, out_weight, out_bias):
    left_wide = left.astype(jnp.float32)
    right_wide = right.astype(jnp.float32)

    def column_block(index):
        start = (index * COL_DEV).astype(jnp.int32)
        block = lax.dynamic_slice_in_dim(right_wide, start, COL_DEV, 1)
        outer = jnp.einsum("sic,sje->ijce", left_wide, block, precision=lax.Precision.HIGHEST) / S
        flat = outer.astype(jnp.bfloat16).reshape(ROWS * COL_DEV, C * C)
        update = jnp.dot(flat, out_weight, preferred_element_type=jnp.float32) + out_bias
        return update.astype(jnp.bfloat16).reshape(ROWS, COL_DEV, PAIR)

    blocks = lax.map(column_block, jnp.arange(N_COL, dtype=jnp.int32))
    return jnp.transpose(blocks, (1, 0, 2, 3)).reshape(ROWS, N_COL * COL_DEV, PAIR)
```

```python
import functools

import jax
import jax.numpy as jnp
from jax import lax
from jax.experimental import pallas as pl
from jax.experimental.pallas import tpu as pltpu
from jax.sharding import PartitionSpec as P


LANES = 128
BF16 = jnp.bfloat16
F32 = jnp.float32
VMEM = pl.BlockSpec(memory_space=pltpu.VMEM)


def tile_update(left_rows, right_cols, out_weight, out_bias):
    seqs, count, width = left_rows.shape
    columns = right_cols.shape[1]
    outer = (
        jnp.einsum("sic,sje->ijce", left_rows, right_cols, preferred_element_type=F32) / seqs
    )
    flat = outer.astype(BF16).reshape(count * columns, width * width)
    update = jnp.dot(flat, out_weight, preferred_element_type=F32) + out_bias
    return update.astype(BF16).reshape(count, columns, out_weight.shape[1])


def rows_update(left_rows, right_cols, out_weight, out_bias):
    seqs, count, width = left_rows.shape
    blocks = jnp.transpose(left_rows.reshape(seqs, count // 8, 8, width), (1, 0, 2, 3))
    results = lax.map(lambda block: tile_update(block, right_cols, out_weight, out_bias), blocks)
    return results.reshape(count, right_cols.shape[1], out_weight.shape[1])


def general(left, right, out_weight, out_bias):
    left_part, right_cols = (
        lax.all_to_all(left, "col", split_axis=1, concat_axis=0, tiled=True),
        lax.all_to_all(right, "col", split_axis=1, concat_axis=0, tiled=True),
    )
    return rows_update(
        lax.all_gather(left_part, "col", axis=1, tiled=True), right_cols, out_weight, out_bias
    )


def turned_order(seqs, width):
    size = seqs * width
    row = lax.broadcasted_iota(jnp.int32, (size, size), 0)
    col = lax.broadcasted_iota(jnp.int32, (size, size), 1)
    return (col == lax.rem(row, seqs) * width + lax.div(row, seqs)).astype(F32).astype(BF16)


def pack_kernel(plan, seqs, width, columns, right_ref, *refs):
    out_refs, turned = refs[:-1], refs[-1]
    chip = lax.div(lax.axis_index("col"), 2)
    order = turned_order(seqs, width)
    total = right_ref.shape[1]
    step = 256
    for start in range(0, total, step):
        block = jnp.dot(order, right_ref[:, start : start + step], preferred_element_type=F32)
        turned[start : start + step, :] = block.astype(BF16).T
    for out_ref, (offset, tiles) in zip(out_refs, plan):
        base = jnp.bitwise_xor(chip, offset // 2) * (2 * columns)
        for core in range(2):
            rows = pl.ds(pl.multiple_of(base + core * columns, 16), columns)
            for place, tile in enumerate(tiles):
                target = (core * len(tiles) + place) * columns
                out_ref[target : target + columns, :] = turned[
                    rows, tile * LANES : (tile + 1) * LANES
                ]


def left_kernel(left_ref, out_ref, wide):
    seqs, count, width = left_ref.shape
    per = LANES // width
    wide[:, :width] = left_ref[...].astype(F32).reshape(seqs * count, width)
    for group in range(count // per):
        for place in range(per):
            piece = wide[pl.ds(group * per + place, seqs, stride=count), :width]
            out_ref[group * seqs : (group + 1) * seqs, place * width : (place + 1) * width] = (
                piece.astype(BF16)
            )


def weight_kernel(width, weight_ref, out_ref, wide):
    wide[...] = weight_ref[...].astype(F32)
    rows = [wide[pl.ds(e, width, stride=width), :] for e in range(width)]
    out_ref[...] = jnp.concatenate(rows, 0).T.astype(BF16)


def unpack(block, filled, source, place, seqs, columns):
    padded = jnp.concatenate([block, jnp.zeros((LANES - columns, LANES), BF16)], 0).T
    per = LANES // seqs
    for e in range(per):
        lanes = slice((place * per + e) * LANES, (place * per + e + 1) * LANES)
        filled[source * seqs : (source + 1) * seqs, lanes] = padded[e * seqs : (e + 1) * seqs, :]


def products(left_ref, weight_ref, filled, tiles, width, per, finish):
    rows = 256
    group = rows // width

    def body(step, carry):
        block = left_ref[pl.ds(pl.multiple_of(step * rows, rows), rows), :]
        totals = [None] * (group // 2)
        for place, tile in enumerate(tiles):
            lanes = slice(place * per * LANES, (place + 1) * per * LANES)
            outer = jnp.dot(block, filled[:, lanes], preferred_element_type=F32).astype(BF16)
            weight = weight_ref[:, tile * per * width : (tile + 1) * per * width]
            for pair in range(group // 2):
                flat = jnp.concatenate(
                    [
                        jnp.concatenate(
                            [
                                outer[
                                    i * width : (i + 1) * width, e * LANES : (e + 1) * LANES
                                ]
                                for e in range(per)
                            ],
                            0,
                        )
                        for i in (2 * pair, 2 * pair + 1)
                    ],
                    1,
                )
                part = jnp.dot(weight, flat, preferred_element_type=F32)
                totals[pair] = part if totals[pair] is None else totals[pair] + part
        for pair in range(group // 2):
            finish(step * (group // 2) + pair, totals[pair])
        return carry

    lax.fori_loop(0, left_ref.shape[0] // rows, body, 0)


def first_kernel(cfg, *refs):
    seqs, columns, width, n, first = cfg
    half = n // 2
    mine = refs[:half]
    other_near, other_far, left_mine, left_other, weight_ref = refs[half : half + 5]
    total_ref, turned_ref, filled = refs[half + 5 :]
    per = LANES // seqs
    core = lax.rem(lax.axis_index("col"), 2)
    groups = turned_ref.shape[0] // LANES
    size = groups * seqs
    for group in range(groups):
        rows = [
            ref[place * size + group * seqs : place * size + (group + 1) * seqs, :]
            for ref in (left_mine, left_other)
            for place in range(half)
        ]
        turned_ref[group * LANES : (group + 1) * LANES, :] = jnp.concatenate(rows, 0).T
    near_rows = other_near.shape[0] // (half // 2)
    far_rows = other_far.shape[0] // (half // 2)
    near_seen = far_seen = 0
    for source, ref in enumerate(mine):
        high = ref.shape[0] // 2
        is_near = high == near_rows
        for place in range(len(first)):
            start = pl.multiple_of(core * high + place * columns, 16)
            unpack(ref[pl.ds(start, columns), :], filled, source, place, seqs, columns)
            other, seen, rows = (
                (other_near, near_seen, near_rows) if is_near else (other_far, far_seen, far_rows)
            )
            start = seen * rows + place * columns
            unpack(
                other[start : start + columns, :], filled, half + source, place, seqs, columns
            )
        if is_near:
            near_seen += 1
        else:
            far_seen += 1

    def finish(index, value):
        total_ref[index] = value

    products(turned_ref, weight_ref, filled, first, width, per, finish)


def last_kernel(cfg, *refs):
    seqs, columns, width, n, first, last = cfg
    half = n // 2
    mine = refs[:half]
    other_near, other_far, turned_ref, weight_ref, total_ref, bias_ref = refs[half : half + 6]
    out_ref, filled = refs[half + 6 :]
    per = LANES // seqs
    core = lax.rem(lax.axis_index("col"), 2)
    near_rows = other_near.shape[0] // (half // 2)
    far_rows = other_far.shape[0] // (half // 2)
    near_seen = far_seen = 0
    for source, ref in enumerate(mine):
        high = ref.shape[0] // 2
        is_near = high == near_rows
        for place in range(len(last)):
            inside = (place + (len(first) if is_near else 0)) * columns
            start = pl.multiple_of(core * high + inside, 16)
            unpack(ref[pl.ds(start, columns), :], filled, source, place, seqs, columns)
            other, seen, rows = (
                (other_near, near_seen, near_rows) if is_near else (other_far, far_seen, far_rows)
            )
            start = seen * rows + inside
            unpack(
                other[start : start + columns, :], filled, half + source, place, seqs, columns
            )
        if is_near:
            near_seen += 1
        else:
            far_seen += 1
    scale = 1.0 / (n * seqs)

    def finish(index, value):
        value = (value + total_ref[index]) * scale
        for place in range(2):
            rows = value[:, place * LANES : (place + 1) * LANES].T[:columns, :]
            out_ref[2 * index + place] = (rows + bias_ref[...]).astype(BF16)

    products(turned_ref, weight_ref, filled, last, width, per, finish)


def fits(left, right, out_weight, n):
    seqs, count, width = left.shape
    columns = right.shape[1] // n
    return (
        n >= 8
        and n & (n - 1) == 0
        and n * seqs == 256
        and width == 32
        and seqs == 16
        and columns % 16 == 0
        and columns <= LANES
        and right.shape[1] % 256 == 0
        and count % 8 == 0
        and out_weight.shape[1] == LANES
    )


def swap(value, distance, n):
    return lax.ppermute(value, "col", [(i, i ^ distance) for i in range(n)])


def fast(n, left, right, out_weight, out_bias):
    seqs, count, width = left.shape
    columns = right.shape[1] // n
    pairs = out_weight.shape[1]
    half = n // 2
    per = LANES // seqs
    tiles = tuple(range(width // per))
    first, last = tiles[:-1], tiles[-1:]
    offsets = [0]
    distance = n // 2
    chain = []
    while distance > 1:
        chain.append(distance)
        offsets = offsets + [o ^ distance for o in offsets]
        distance //= 2
    far = [o for o in offsets if o & (n // 2)]
    near = [o for o in offsets if not o & (n // 2)]
    plan = [(o, first) for o in far] + [(o, tiles) for o in near] + [(o, last) for o in far]
    flat_right = jnp.transpose(right, (0, 2, 1)).reshape(seqs * width, right.shape[1])
    shape = lambda rows: jax.ShapeDtypeStruct((rows, LANES), BF16)
    packed = pl.pallas_call(
        functools.partial(pack_kernel, plan, seqs, width, columns),
        out_shape=[shape(2 * len(t) * columns) for _, t in plan],
        in_specs=[VMEM],
        out_specs=[VMEM] * len(plan),
        scratch_shapes=[pltpu.VMEM((right.shape[1], seqs * width), BF16)],
        name="pack",
    )(flat_right)
    send = {(o, t): value for (o, t), value in zip(plan, packed)}
    left_block = pl.pallas_call(
        left_kernel,
        out_shape=shape(count * width // LANES * seqs),
        in_specs=[VMEM],
        out_specs=VMEM,
        scratch_shapes=[pltpu.VMEM((seqs * count, LANES), F32)],
        name="left_pack",
    )(left)
    turned_weight = pl.pallas_call(
        functools.partial(weight_kernel, width),
        out_shape=jax.ShapeDtypeStruct((pairs, width * width), BF16),
        in_specs=[VMEM],
        out_specs=VMEM,
        scratch_shapes=[pltpu.VMEM((width * width, pairs), F32)],
        name="weight_pack",
    )(out_weight)

    got = {}
    for o in far:
        got[o, first] = swap(send[o, first], o, n)
    for o in near:
        got[o, tiles] = swap(send[o, tiles], o, n) if o else send[o, tiles]
    for o in far:
        got[o, last] = swap(send[o, last], o, n)
    lefts = left_block
    for distance in chain:
        lefts = jnp.concatenate([lefts, swap(lefts, distance, n)], 0)
    other_lefts = swap(lefts, 1, n)

    other_core = 1 - lax.rem(lax.axis_index("col"), 2)

    def exchange(keys):
        parts = []
        for key in keys:
            rows = got[key].shape[0] // 2
            parts.append(lax.dynamic_slice_in_dim(got[key], other_core * rows, rows, 0))
        return swap(jnp.concatenate(parts, 0), 1, n)

    other_near = exchange([(o, tiles) for o in near])
    other_far_first = exchange([(o, first) for o in far])
    other_far_last = exchange([(o, last) for o in far])

    key_first = [(o, first) if o in far else (o, tiles) for o in offsets]
    key_last = [(o, last) if o in far else (o, tiles) for o in offsets]
    cells = n * seqs
    total, turned_left = pl.pallas_call(
        functools.partial(first_kernel, (seqs, columns, width, n, first)),
        out_shape=[
            jax.ShapeDtypeStruct((count // 2, pairs, 2 * LANES), F32),
            jax.ShapeDtypeStruct((count * width, cells), BF16),
        ],
        in_specs=[VMEM] * (half + 5),
        out_specs=[VMEM] * 2,
        scratch_shapes=[pltpu.VMEM((cells, len(first) * per * LANES), BF16)],
        name="first",
    )(
        *[got[k] for k in key_first],
        other_near,
        other_far_first,
        lefts,
        other_lefts,
        turned_weight,
    )
    return pl.pallas_call(
        functools.partial(last_kernel, (seqs, columns, width, n, first, last)),
        out_shape=jax.ShapeDtypeStruct((count, columns, pairs), BF16),
        in_specs=[VMEM] * (half + 6),
        out_specs=VMEM,
        scratch_shapes=[pltpu.VMEM((cells, len(last) * per * LANES), BF16)],
        name="last",
    )(
        *[got[k] for k in key_last],
        other_near,
        other_far_last,
        turned_left,
        turned_weight,
        total,
        out_bias.reshape(1, pairs),
    )


def solution(mesh):
    n = mesh.shape["col"]

    def on_device(left, right, out_weight, out_bias):
        if fits(left, right, out_weight, n):
            return fast(n, left, right, out_weight, out_bias)
        return general(left, right, out_weight, out_bias)

    in_specs = (P("col", "groups", None), P("col", "groups", None), P(), P())
    out_specs = P("groups", "col", None)
    return jax.shard_map(
        on_device, mesh=mesh, in_specs=in_specs, out_specs=out_specs, check_vma=False
    )
```

```python
import functools

import jax
import jax.numpy as jnp
from jax import lax
from jax.experimental import pallas as pl
from jax.experimental.pallas import tpu as pltpu
from jax.sharding import PartitionSpec as P


LANES = 128
FIRST = 2
BF16 = jnp.bfloat16
F32 = jnp.float32
VMEM = pl.BlockSpec(memory_space=pltpu.VMEM)


def tile_update(left_rows, right_cols, out_weight, out_bias):
    seqs, count, width = left_rows.shape
    columns = right_cols.shape[1]
    outer = (
        jnp.einsum("sic,sje->ijce", left_rows, right_cols, preferred_element_type=F32) / seqs
    )
    flat = outer.astype(BF16).reshape(count * columns, width * width)
    update = jnp.dot(flat, out_weight, preferred_element_type=F32) + out_bias
    return update.astype(BF16).reshape(count, columns, out_weight.shape[1])


def rows_update(left_rows, right_cols, out_weight, out_bias):
    seqs, count, width = left_rows.shape
    blocks = jnp.transpose(left_rows.reshape(seqs, count // 8, 8, width), (1, 0, 2, 3))
    results = lax.map(lambda block: tile_update(block, right_cols, out_weight, out_bias), blocks)
    return results.reshape(count, right_cols.shape[1], out_weight.shape[1])


def general(left, right, out_weight, out_bias):
    left_part, right_cols = (
        lax.all_to_all(left, "col", split_axis=1, concat_axis=0, tiled=True),
        lax.all_to_all(right, "col", split_axis=1, concat_axis=0, tiled=True),
    )
    return rows_update(
        lax.all_gather(left_part, "col", axis=1, tiled=True), right_cols, out_weight, out_bias
    )


def turned_order(seqs, width):
    size = seqs * width
    row = lax.broadcasted_iota(jnp.int32, (size, size), 0)
    col = lax.broadcasted_iota(jnp.int32, (size, size), 1)
    return (col == lax.rem(row, seqs) * width + lax.div(row, seqs)).astype(F32).astype(BF16)


def half_start(span, columns, flip):
    upper = lax.div(lax.div(lax.axis_index("col"), 2) * (2 * columns), span)
    return pl.multiple_of((1 - upper if flip else upper) * span, LANES)


def pieces(total):
    return [(begin, min(2 * LANES, total - begin)) for begin in range(0, total, 2 * LANES)]


def turn(source, turned, order, begin, step):
    block = jnp.dot(order, source[:, begin : begin + step], preferred_element_type=F32)
    turned[begin : begin + step, :] = block.astype(BF16).T


def put_core(out_ref, at, turned, offset, start, core, tiles, columns):
    chip = lax.div(lax.axis_index("col"), 2)
    base = jnp.bitwise_xor(chip, lax.div(offset, 2)) * (2 * columns) - start
    rows = pl.ds(pl.multiple_of(base + core * columns, 16), columns)
    for place, tile in enumerate(tiles):
        target = at + place * columns
        out_ref[target : target + columns, :] = turned[rows, tile * LANES : (tile + 1) * LANES]


def put(out_ref, turned, offset, start, tiles, columns):
    for core in range(2):
        at = core * len(tiles) * columns
        put_core(out_ref, at, turned, offset, start, core, tiles, columns)


def put_all(units, turned, start, keep_refs, give_refs, columns):
    core = lax.rem(lax.axis_index("col"), 2)
    for (base, step, tiles), keep, give in zip(units, keep_refs, give_refs):
        put(keep, turned, base + step * core, start, tiles, columns)
        if step:
            put(give, turned, base + step * (1 - core), start, tiles, columns)


def pack_left(left, out_ref, wide):
    seqs, count, width = left.shape
    per = LANES // width
    wide[:, :width] = left[...].astype(F32).reshape(seqs * count, width)
    for group in range(count // per):
        for place in range(per):
            piece = wide[pl.ds(group * per + place, seqs, stride=count), :width]
            out_ref[group * seqs : (group + 1) * seqs, place * width : (place + 1) * width] = (
                piece.astype(BF16)
            )


def read_kernel(columns, right_ref, left_ref, far_out, left_out, left, wide, sems):
    span = far_out.shape[1]
    far = right_ref.at[:, pl.ds(half_start(span, columns, True), span)]
    copies = [
        pltpu.make_async_copy(left_ref, left, sems.at[0]),
        pltpu.make_async_copy(far, far_out, sems.at[1]),
    ]
    for copy in copies:
        copy.start()
    copies[0].wait()
    pack_left(left, left_out, wide)
    copies[1].wait()


def far_kernel(cfg, far_ref, *refs):
    seqs, width, columns, units, (base, step, tiles) = cfg
    keeps, gives = refs[: len(units)], refs[len(units) : 2 * len(units)]
    *singles, turned = refs[2 * len(units) :]
    order = turned_order(seqs, width)
    for begin, size in pieces(turned.shape[0]):
        turn(far_ref, turned, order, begin, size)
    start = half_start(turned.shape[0], columns, True)
    put_all(units, turned, start, keeps, gives, columns)
    core = lax.rem(lax.axis_index("col"), 2)
    for place, ref in enumerate(singles):
        flip, offset = place % 2, base + step * (place // 2)
        put_core(ref, 0, turned, offset, start, jnp.bitwise_xor(core, flip), tiles, columns)


def near_kernel(cfg, right_ref, weight_ref, *refs):
    seqs, width, columns, units, pairs = cfg
    keeps, gives = refs[: len(units)], refs[len(units) : len(units) + pairs]
    weight_out, near, turned, raw, wide, sems = refs[len(units) + pairs :]
    start = half_start(turned.shape[0], columns, False)
    copies = [
        pltpu.make_async_copy(weight_ref, raw, sems.at[0]),
        pltpu.make_async_copy(right_ref.at[:, pl.ds(start, near.shape[1])], near, sems.at[1]),
    ]
    for copy in copies:
        copy.start()
    order = turned_order(seqs, width)
    copies[0].wait()
    wide[...] = raw[...].astype(F32)
    rows = [wide[pl.ds(e, width, stride=width), :] for e in range(width)]
    weight_out[...] = jnp.concatenate(rows, 0).T.astype(BF16)
    copies[1].wait()
    for begin, step in pieces(turned.shape[0]):
        turn(near, turned, order, begin, step)
    given = iter(gives)
    places = [next(given) if step else None for _, step, _ in units]
    put_all(units, turned, start, keeps, places, columns)


def unpack(block, filled, position, place, seqs, columns):
    padded = jnp.concatenate([block, jnp.zeros((LANES - columns, LANES), BF16)], 0).T
    per = LANES // seqs
    rows = pl.ds(pl.multiple_of(position * seqs, 16), seqs)
    for e in range(per):
        lanes = slice((place * per + e) * LANES, (place * per + e + 1) * LANES)
        filled[rows, lanes] = padded[e * seqs : (e + 1) * seqs, :]


def fill(units, tiles, offsets, mine, other, filled, seqs, columns):
    half = len(offsets[0])
    core = lax.rem(lax.axis_index("col"), 2)

    def at(swapped, distance, step=0):
        ends = (distance, distance + step) if step >= 0 else (distance - step, distance)
        first, second = (1, 0) if swapped else (0, 1)
        place = jnp.where(
            core == 0, offsets[first].index(ends[0]), offsets[second].index(ends[1])
        )
        return place + half if swapped else place

    other = iter(other)
    for (base, step, held), own in zip(units, mine):
        passed = None if len(own) == 4 else next(other)
        high = len(held) * columns
        two = 2 * high if len(own) == 1 else 0
        direct = len(own) == 4
        for place, tile in enumerate(tiles):
            inside = held.index(tile) * columns
            if direct:
                blocks = [
                    (ref, inside, at(bool(k % 2), base + step * (k // 2)))
                    for k, ref in enumerate(own)
                ]
            elif step:
                blocks = [
                    (own[0], core * high + inside, at(False, base, step)),
                    (own[-1], two + core * high + inside, at(True, base, step)),
                    (passed, inside, at(True, base, -step)),
                    (passed, high + inside, at(False, base, -step)),
                ]
            else:
                blocks = [
                    (own[0], core * high + inside, at(False, base)),
                    (passed, inside, at(True, base)),
                ]
            for ref, start, position in blocks:
                block = ref[pl.ds(pl.multiple_of(start, 16), columns), :]
                unpack(block, filled, position, place, seqs, columns)


def by_unit(refs, counts):
    mine = []
    for count in counts:
        mine.append(refs[:count])
        refs = refs[count:]
    passed = sum(count < 4 for count in counts)
    return mine, refs[:passed], refs[passed:]


def products(left_ref, weight_ref, filled, tiles, width, per, finish, after=None):
    rows = 256
    group = rows // width

    def body(step):
        block = left_ref[step * rows : (step + 1) * rows, :]
        totals = [None] * (group // 2)
        for place, tile in enumerate(tiles):
            lanes = slice(place * per * LANES, (place + 1) * per * LANES)
            outer = jnp.dot(block, filled[:, lanes], preferred_element_type=F32).astype(BF16)
            weight = weight_ref[:, tile * per * width : (tile + 1) * per * width]
            for pair in range(group // 2):
                flat = jnp.concatenate(
                    [
                        jnp.concatenate(
                            [
                                outer[
                                    i * width : (i + 1) * width, e * LANES : (e + 1) * LANES
                                ]
                                for e in range(per)
                            ],
                            0,
                        )
                        for i in (2 * pair, 2 * pair + 1)
                    ],
                    1,
                )
                part = jnp.dot(weight, flat, preferred_element_type=F32)
                totals[pair] = part if totals[pair] is None else totals[pair] + part
        for pair in range(group // 2):
            finish(step * (group // 2) + pair, totals[pair])
        if after is not None:
            after(step)

    for step in range(left_ref.shape[0] // rows):
        body(step)


def first_kernel(cfg, *refs):
    seqs, columns, width, units, counts, offsets, tiles = cfg
    mine, other, refs = by_unit(refs, counts)
    left_mine, left_other, weight_ref, total_ref, turned_ref, filled = refs
    groups = turned_ref.shape[0] // LANES
    size = groups * seqs
    for group in range(groups):
        rows = [
            ref[place * size + group * seqs : place * size + (group + 1) * seqs, :]
            for ref in (left_mine, left_other)
            for place in range(len(offsets[0]))
        ]
        turned_ref[group * LANES : (group + 1) * LANES, :] = jnp.concatenate(rows, 0).T
    fill(units, tiles, offsets, mine, other, filled, seqs, columns)

    def finish(index, value):
        total_ref[index] = value

    products(turned_ref, weight_ref, filled, tiles, width, LANES // seqs, finish)


def last_kernel(cfg, *refs):
    seqs, columns, width, units, counts, offsets, tiles = cfg
    mine, other, refs = by_unit(refs, counts)
    turned_ref, weight_ref, total_ref, bias_ref, out_ref, filled, ready, sems = refs
    fill(units, tiles, offsets, mine, other, filled, seqs, columns)
    scale = 1.0 / (2 * len(offsets[0]) * seqs)

    def finish(index, value):
        value = (value + total_ref[index]) * scale
        for place in range(2):
            rows = value[:, place * LANES : (place + 1) * LANES].T[:columns, :]
            ready[2 * index + place] = (rows + bias_ref[...]).astype(BF16)

    def write(step, rows):
        at = pl.ds(step * rows, rows)
        return pltpu.make_async_copy(ready.at[at], out_ref.at[at], sems.at[step])

    steps = sems.shape[0]
    rows = ready.shape[0] // steps
    per = LANES // seqs
    products(
        turned_ref, weight_ref, filled, tiles, width, per, finish,
        lambda step: write(step, rows).start(),
    )
    for step in range(steps):
        write(step, rows).wait()


def fits(left, right, out_weight, n):
    seqs, count, width = left.shape
    columns = right.shape[1] // n
    return (
        n >= 8
        and n & (n - 1) == 0
        and n * seqs == 256
        and width == 32
        and seqs == 16
        and columns % 16 == 0
        and columns <= LANES
        and right.shape[1] % (2 * LANES) == 0
        and count % 8 == 0
        and out_weight.shape[1] == LANES
    )


def swap(value, distance, n, by_core=0):
    return lax.ppermute(value, "col", [(i, i ^ (distance + by_core * (i & 1))) for i in range(n)])


def fast(n, left, right, out_weight, out_bias):
    seqs, count, width = left.shape
    columns = right.shape[1] // n
    pairs = out_weight.shape[1]
    per = LANES // seqs
    cells = n * seqs
    span = right.shape[1] // 2
    tiles = tuple(range(width // per))
    first, last = tiles[:FIRST], tiles[FIRST:]
    offsets = ([0], [0])
    chain = []
    distance = n // 2
    while distance > 1:
        step = n // 4 if distance == n // 2 else 0
        chain.append((distance, step))
        offsets = tuple(
            have + [o ^ (distance + step * core) for o in have]
            for core, have in enumerate(offsets)
        )
        distance //= 2
    far = [b for b in range(n // 2, n, 2) if not b & (n // 4)]
    near = [(b, 2, tiles) for b in range(4, n // 2, 4)]
    near += [(2, 0, tiles), (0, 0, tiles)]
    far_whole = [(b, n // 4, tiles) for b in far[:-1]]
    far_first = far_whole + [(far[-1], n // 4, first)]
    far_last = (far[-1], n // 4, last)
    shape = lambda rows: jax.ShapeDtypeStruct((rows, LANES), BF16)
    high = lambda unit: 2 * len(unit[2]) * columns
    in_hbm = lambda x: pltpu.with_memory_space_constraint(x, pltpu.MemorySpace.HBM)
    params = lambda mib: pltpu.CompilerParams(vmem_limit_bytes=mib << 20)
    flat_right = jnp.transpose(right, (0, 2, 1)).reshape(seqs * width, right.shape[1])
    anywhere = pl.BlockSpec(memory_space=pl.ANY)
    right_hbm = in_hbm(flat_right)
    far_right, left_block = pl.pallas_call(
        functools.partial(read_kernel, columns),
        out_shape=[
            jax.ShapeDtypeStruct((seqs * width, span), BF16),
            shape(count * width // LANES * seqs),
        ],
        in_specs=[anywhere] * 2,
        out_specs=[VMEM] * 2,
        scratch_shapes=[
            pltpu.VMEM(left.shape, BF16),
            pltpu.VMEM((seqs * count, LANES), F32),
            pltpu.SemaphoreType.DMA((2,)),
        ],
        compiler_params=params(6),
        name="read",
    )(right_hbm, in_hbm(left))
    packed = pl.pallas_call(
        functools.partial(far_kernel, (seqs, width, columns, far_first, far_last)),
        out_shape=[shape(high(u)) for u in far_first * 2] + [shape(high(far_last) // 2)] * 4,
        in_specs=[VMEM],
        out_specs=[VMEM] * (2 * len(far_first) + 4),
        scratch_shapes=[pltpu.VMEM((span, seqs * width), BF16)],
        compiler_params=params(10),
        name="pack_far",
    )(far_right)
    keep = dict(zip(far_first, packed))
    give = dict(zip(far_first, packed[len(far_first) :]))
    singles = packed[2 * len(far_first) :]
    near_pairs = [u for u in near if u[1]]
    packed = pl.pallas_call(
        functools.partial(near_kernel, (seqs, width, columns, near, len(near_pairs))),
        out_shape=[shape(high(u)) for u in near + near_pairs]
        + [jax.ShapeDtypeStruct((pairs, width * width), BF16)],
        in_specs=[anywhere] * 2,
        out_specs=[VMEM] * (len(near + near_pairs) + 1),
        scratch_shapes=[
            pltpu.VMEM((seqs * width, span), BF16),
            pltpu.VMEM((span, seqs * width), BF16),
            pltpu.VMEM(out_weight.shape, BF16),
            pltpu.VMEM((width * width, pairs), F32),
            pltpu.SemaphoreType.DMA((2,)),
        ],
        compiler_params=params(10),
        name="pack_near",
    )(right_hbm, in_hbm(out_weight))
    keep.update(zip(near, packed))
    give.update(zip(near_pairs, packed[len(near) :]))
    turned_weight = packed[-1]

    got = {}

    for units in (far_first, near):
        for unit in units:
            base, step, _ = unit
            value = keep[unit]
            if step:
                theirs = swap(give[unit], 1, n)
                if unit == far_first[0]:
                    got[unit] = [swap(value, base, n, step), swap(theirs, base, n, step)]
                    continue
                value = jnp.concatenate([value, theirs], 0)
            got[unit] = [swap(value, base, n, step) if base else value]
    got[far_last] = []
    for place, value in enumerate(singles):
        distance = far_last[0] + far_last[1] * (place // 2) + place % 2
        got[far_last].append(swap(value, distance, n))
    lefts = left_block
    for distance, step in chain:
        got_left = swap(lefts, distance, n, step)
        lefts = jnp.concatenate([lefts, got_left], 0)
    other_lefts = swap(lefts, 1, n)

    other_core = 1 - lax.rem(lax.axis_index("col"), 2)
    passed = {}
    for units in (near, far_first):
        for unit in units:
            halves = []
            for value in got[unit]:
                parts = value.reshape(-1, 2, high(unit) // 2, LANES)
                half = lax.dynamic_slice_in_dim(parts, other_core, 1, 1)
                halves.append(half.reshape(-1, LANES))
            half = jnp.concatenate(halves, 0) if len(halves) > 1 else halves[0]
            passed[unit] = swap(half, 1, n)

    units = far_first + near
    counts = [len(got[u]) for u in units]
    total, turned_left = pl.pallas_call(
        functools.partial(first_kernel, (seqs, columns, width, units, counts, offsets, first)),
        out_shape=[
            jax.ShapeDtypeStruct((count // 2, pairs, 2 * LANES), F32),
            jax.ShapeDtypeStruct((count * width, cells), BF16),
        ],
        in_specs=[VMEM] * (sum(counts) + len(units) + 3),
        out_specs=[VMEM] * 2,
        scratch_shapes=[pltpu.VMEM((cells, len(first) * per * LANES), BF16)],
        compiler_params=params(24),
        name="first",
    )(*[v for u in units for v in got[u]], *[passed[u] for u in units], lefts, other_lefts, turned_weight)
    units = far_whole + [far_last] + near
    held = [passed[u] for u in units if u in passed]
    counts = [len(got[u]) for u in units]
    return pl.pallas_call(
        functools.partial(last_kernel, (seqs, columns, width, units, counts, offsets, last)),
        out_shape=jax.ShapeDtypeStruct((count, columns, pairs), BF16),
        in_specs=[VMEM] * (sum(counts) + len(held) + 4),
        out_specs=pl.BlockSpec(memory_space=pl.ANY),
        scratch_shapes=[
            pltpu.VMEM((cells, len(last) * per * LANES), BF16),
            pltpu.VMEM((count, columns, pairs), BF16),
            pltpu.SemaphoreType.DMA((count * width // 256,)),
        ],
        compiler_params=params(24),
        name="last",
    )(
        *[v for u in units for v in got[u]],
        *held,
        turned_left,
        turned_weight,
        total,
        out_bias.reshape(1, pairs),
    )


def solution(mesh):
    n = mesh.shape["col"]

    def on_device(left, right, out_weight, out_bias):
        if fits(left, right, out_weight, n):
            return fast(n, left, right, out_weight, out_bias)
        return general(left, right, out_weight, out_bias)

    in_specs = (P("col", "groups", None), P("col", "groups", None), P(), P())
    out_specs = P("groups", "col", None)
    return jax.shard_map(
        on_device, mesh=mesh, in_specs=in_specs, out_specs=out_specs, check_vma=False
    )
```

```python
import functools

import jax
import jax.numpy as jnp
from jax import lax
from jax.experimental import pallas as pl
from jax.experimental.pallas import tpu as pltpu
from jax.sharding import PartitionSpec as P


LANES = 128
FIRST = 2
ROWS = 512
BF16 = jnp.bfloat16
F32 = jnp.float32
VMEM = pl.BlockSpec(memory_space=pltpu.VMEM)


def tile_update(left_rows, right_cols, out_weight, out_bias):
    seqs, count, width = left_rows.shape
    columns = right_cols.shape[1]
    outer = (
        jnp.einsum("sic,sje->ijce", left_rows, right_cols, preferred_element_type=F32) / seqs
    )
    flat = outer.astype(BF16).reshape(count * columns, width * width)
    update = jnp.dot(flat, out_weight, preferred_element_type=F32) + out_bias
    return update.astype(BF16).reshape(count, columns, out_weight.shape[1])


def rows_update(left_rows, right_cols, out_weight, out_bias):
    seqs, count, width = left_rows.shape
    blocks = jnp.transpose(left_rows.reshape(seqs, count // 8, 8, width), (1, 0, 2, 3))
    results = lax.map(lambda block: tile_update(block, right_cols, out_weight, out_bias), blocks)
    return results.reshape(count, right_cols.shape[1], out_weight.shape[1])


def general(left, right, out_weight, out_bias):
    left_part, right_cols = (
        lax.all_to_all(left, "col", split_axis=1, concat_axis=0, tiled=True),
        lax.all_to_all(right, "col", split_axis=1, concat_axis=0, tiled=True),
    )
    return rows_update(
        lax.all_gather(left_part, "col", axis=1, tiled=True), right_cols, out_weight, out_bias
    )


def turned_order(seqs, width):
    size = seqs * width
    row = lax.broadcasted_iota(jnp.int32, (size, size), 0)
    col = lax.broadcasted_iota(jnp.int32, (size, size), 1)
    return (col == lax.rem(row, seqs) * width + lax.div(row, seqs)).astype(F32).astype(BF16)


def half_start(span, columns, flip):
    upper = lax.div(lax.div(lax.axis_index("col"), 2) * (2 * columns), span)
    return pl.multiple_of((1 - upper if flip else upper) * span, LANES)


def pieces(total):
    return [(begin, min(2 * LANES, total - begin)) for begin in range(0, total, 2 * LANES)]


def turn(source, turned, order, begin, step):
    block = jnp.dot(order, source[:, begin : begin + step], preferred_element_type=F32)
    turned[begin : begin + step, :] = block.astype(BF16).T


def put_core(out_ref, at, turned, offset, start, core, tiles, columns):
    chip = lax.div(lax.axis_index("col"), 2)
    base = jnp.bitwise_xor(chip, lax.div(offset, 2)) * (2 * columns) - start
    rows = pl.ds(pl.multiple_of(base + core * columns, 16), columns)
    for place, tile in enumerate(tiles):
        target = at + place * columns
        out_ref[target : target + columns, :] = turned[rows, tile * LANES : (tile + 1) * LANES]


def put(out_ref, turned, offset, start, tiles, columns):
    for core in range(2):
        at = core * len(tiles) * columns
        put_core(out_ref, at, turned, offset, start, core, tiles, columns)


def put_all(units, turned, start, keep_refs, give_refs, columns):
    core = lax.rem(lax.axis_index("col"), 2)
    for (base, step, tiles), keep, give in zip(units, keep_refs, give_refs):
        put(keep, turned, base + step * core, start, tiles, columns)
        if step:
            put(give, turned, base + step * (1 - core), start, tiles, columns)


def pack_left(left, out_ref, wide):
    seqs, count, width = left.shape
    per = LANES // width
    wide[:, :width] = left[...].astype(F32).reshape(seqs * count, width)
    for group in range(count // per):
        for place in range(per):
            piece = wide[pl.ds(group * per + place, seqs, stride=count), :width]
            out_ref[group * seqs : (group + 1) * seqs, place * width : (place + 1) * width] = (
                piece.astype(BF16)
            )


def read_kernel(columns, right_ref, left_ref, far_out, left_out, left, wide, sems):
    span = far_out.shape[1]
    far = right_ref.at[:, pl.ds(half_start(span, columns, True), span)]
    copies = [
        pltpu.make_async_copy(left_ref, left, sems.at[0]),
        pltpu.make_async_copy(far, far_out, sems.at[1]),
    ]
    for copy in copies:
        copy.start()
    copies[0].wait()
    pack_left(left, left_out, wide)
    copies[1].wait()


def far_kernel(cfg, far_ref, *refs):
    seqs, width, columns, units, (base, step, tiles) = cfg
    keeps, gives = refs[: len(units)], refs[len(units) : 2 * len(units)]
    *singles, turned = refs[2 * len(units) :]
    order = turned_order(seqs, width)
    for begin, size in pieces(turned.shape[0]):
        turn(far_ref, turned, order, begin, size)
    start = half_start(turned.shape[0], columns, True)
    put_all(units, turned, start, keeps, gives, columns)
    core = lax.rem(lax.axis_index("col"), 2)
    for place, ref in enumerate(singles):
        flip, offset = place % 2, base + step * (place // 2)
        put_core(ref, 0, turned, offset, start, jnp.bitwise_xor(core, flip), tiles, columns)


def near_kernel(cfg, right_ref, weight_ref, *refs):
    seqs, width, columns, units, pairs = cfg
    keeps, gives = refs[: len(units)], refs[len(units) : len(units) + pairs]
    weight_out, near, turned, raw, wide, sems = refs[len(units) + pairs :]
    start = half_start(turned.shape[0], columns, False)
    copies = [
        pltpu.make_async_copy(weight_ref, raw, sems.at[0]),
        pltpu.make_async_copy(right_ref.at[:, pl.ds(start, near.shape[1])], near, sems.at[1]),
    ]
    for copy in copies:
        copy.start()
    order = turned_order(seqs, width)
    copies[0].wait()
    wide[...] = raw[...].astype(F32)
    rows = [wide[pl.ds(e, width, stride=width), :] for e in range(width)]
    weight_out[...] = jnp.concatenate(rows, 0).T.astype(BF16)
    copies[1].wait()
    for begin, step in pieces(turned.shape[0]):
        turn(near, turned, order, begin, step)
    given = iter(gives)
    places = [next(given) if step else None for _, step, _ in units]
    put_all(units, turned, start, keeps, places, columns)


def unpack(block, filled, position, place, seqs, columns):
    padded = jnp.concatenate([block, jnp.zeros((LANES - columns, LANES), BF16)], 0).T
    per = LANES // seqs
    rows = pl.ds(pl.multiple_of(position * seqs, 16), seqs)
    for e in range(per):
        lanes = slice((place * per + e) * LANES, (place * per + e + 1) * LANES)
        filled[rows, lanes] = padded[e * seqs : (e + 1) * seqs, :]


def fill(units, tiles, offsets, mine, other, filled, seqs, columns):
    half = len(offsets[0])
    core = lax.rem(lax.axis_index("col"), 2)

    def at(swapped, distance, step=0):
        ends = (distance, distance + step) if step >= 0 else (distance - step, distance)
        first, second = (1, 0) if swapped else (0, 1)
        place = jnp.where(
            core == 0, offsets[first].index(ends[0]), offsets[second].index(ends[1])
        )
        return place + half if swapped else place

    other = iter(other)
    for (base, step, held), own in zip(units, mine):
        passed = None if len(own) == 4 else next(other)
        high = len(held) * columns
        two = 2 * high if len(own) == 1 else 0
        direct = len(own) == 4
        for place, tile in enumerate(tiles):
            inside = held.index(tile) * columns
            if direct:
                blocks = [
                    (ref, inside, at(bool(k % 2), base + step * (k // 2)))
                    for k, ref in enumerate(own)
                ]
            elif step:
                blocks = [
                    (own[0], core * high + inside, at(False, base, step)),
                    (own[-1], two + core * high + inside, at(True, base, step)),
                    (passed, inside, at(True, base, -step)),
                    (passed, high + inside, at(False, base, -step)),
                ]
            else:
                blocks = [
                    (own[0], core * high + inside, at(False, base)),
                    (passed, inside, at(True, base)),
                ]
            for ref, start, position in blocks:
                block = ref[pl.ds(pl.multiple_of(start, 16), columns), :]
                unpack(block, filled, position, place, seqs, columns)


def by_unit(refs, counts):
    mine = []
    for count in counts:
        mine.append(refs[:count])
        refs = refs[count:]
    passed = sum(count < 4 for count in counts)
    return mine, refs[:passed], refs[passed:]


def products(left_ref, weight_ref, filled, tiles, width, per, finish):
    rows = ROWS if left_ref.shape[0] % ROWS == 0 else 256
    group = rows // width
    steps = left_ref.shape[0] // rows
    spots = [(step, place) for step in range(steps) for place in range(len(tiles))]

    def outer_of(step, place):
        block = left_ref[step * rows : (step + 1) * rows, :]
        lanes = slice(place * per * LANES, (place + 1) * per * LANES)
        return jnp.dot(block, filled[:, lanes], preferred_element_type=F32).astype(BF16)

    ahead = outer_of(*spots[0])
    totals = [None] * (group // 2)
    for at, (step, place) in enumerate(spots):
        outer = ahead
        if at + 1 < len(spots):
            ahead = outer_of(*spots[at + 1])
        tile = tiles[place]
        weight = weight_ref[:, tile * per * width : (tile + 1) * per * width]
        for pair in range(group // 2):
            flat = jnp.concatenate(
                [
                    jnp.concatenate(
                        [
                            outer[i * width : (i + 1) * width, e * LANES : (e + 1) * LANES]
                            for e in range(per)
                        ],
                        0,
                    )
                    for i in (2 * pair, 2 * pair + 1)
                ],
                1,
            )
            part = jnp.dot(weight, flat, preferred_element_type=F32)
            totals[pair] = part if place == 0 else totals[pair] + part
        if place == len(tiles) - 1:
            for pair in range(group // 2):
                finish(step * (group // 2) + pair, totals[pair])


def first_kernel(cfg, *refs):
    seqs, columns, width, units, counts, offsets, tiles = cfg
    mine, other, refs = by_unit(refs, counts)
    left_mine, left_other, weight_ref, total_ref, turned_ref, filled = refs
    groups = turned_ref.shape[0] // LANES
    size = groups * seqs
    for group in range(groups):
        rows = [
            ref[place * size + group * seqs : place * size + (group + 1) * seqs, :]
            for ref in (left_mine, left_other)
            for place in range(len(offsets[0]))
        ]
        turned_ref[group * LANES : (group + 1) * LANES, :] = jnp.concatenate(rows, 0).T
    fill(units, tiles, offsets, mine, other, filled, seqs, columns)

    def finish(index, value):
        total_ref[index] = value

    products(turned_ref, weight_ref, filled, tiles, width, LANES // seqs, finish)


def last_kernel(cfg, *refs):
    seqs, columns, width, units, counts, offsets, tiles = cfg
    mine, other, refs = by_unit(refs, counts)
    turned_ref, weight_ref, total_ref, bias_ref, out_ref, filled, ready, sems = refs
    fill(units, tiles, offsets, mine, other, filled, seqs, columns)
    scale = 1.0 / (2 * len(offsets[0]) * seqs)

    def write(index):
        at = pl.ds(2 * index, 2)
        return pltpu.make_async_copy(ready.at[at], out_ref.at[at], sems.at[index])

    def finish(index, value):
        value = (value + total_ref[index]) * scale
        for place in range(2):
            rows = value[:, place * LANES : (place + 1) * LANES].T[:columns, :]
            ready[2 * index + place] = (rows + bias_ref[...]).astype(BF16)
        write(index).start()

    products(turned_ref, weight_ref, filled, tiles, width, LANES // seqs, finish)
    for index in range(sems.shape[0]):
        write(index).wait()


def fits(left, right, out_weight, n):
    seqs, count, width = left.shape
    columns = right.shape[1] // n
    return (
        n >= 8
        and n & (n - 1) == 0
        and n * seqs == 256
        and width == 32
        and seqs == 16
        and columns % 16 == 0
        and columns <= LANES
        and right.shape[1] % (2 * LANES) == 0
        and count % 8 == 0
        and out_weight.shape[1] == LANES
    )


def swap(value, distance, n, by_core=0):
    return lax.ppermute(value, "col", [(i, i ^ (distance + by_core * (i & 1))) for i in range(n)])


def fast(n, left, right, out_weight, out_bias):
    seqs, count, width = left.shape
    columns = right.shape[1] // n
    pairs = out_weight.shape[1]
    per = LANES // seqs
    cells = n * seqs
    span = right.shape[1] // 2
    tiles = tuple(range(width // per))
    first, last = tiles[:FIRST], tiles[FIRST:]
    offsets = ([0], [0])
    chain = []
    distance = n // 2
    while distance > 1:
        step = n // 4 if distance == n // 2 else 0
        chain.append((distance, step))
        offsets = tuple(
            have + [o ^ (distance + step * core) for o in have]
            for core, have in enumerate(offsets)
        )
        distance //= 2
    far = [b for b in range(n // 2, n, 2) if not b & (n // 4)]
    near = [(b, 2, tiles) for b in range(4, n // 2, 4)]
    near += [(2, 0, tiles), (0, 0, tiles)]
    far_whole = [(b, n // 4, tiles) for b in far[:-1]]
    far_first = far_whole + [(far[-1], n // 4, first)]
    far_last = (far[-1], n // 4, last)
    shape = lambda rows: jax.ShapeDtypeStruct((rows, LANES), BF16)
    high = lambda unit: 2 * len(unit[2]) * columns
    in_hbm = lambda x: pltpu.with_memory_space_constraint(x, pltpu.MemorySpace.HBM)
    params = lambda mib: pltpu.CompilerParams(vmem_limit_bytes=mib << 20)
    flat_right = jnp.transpose(right, (0, 2, 1)).reshape(seqs * width, right.shape[1])
    anywhere = pl.BlockSpec(memory_space=pl.ANY)
    right_hbm = in_hbm(flat_right)
    far_right, left_block = pl.pallas_call(
        functools.partial(read_kernel, columns),
        out_shape=[
            jax.ShapeDtypeStruct((seqs * width, span), BF16),
            shape(count * width // LANES * seqs),
        ],
        in_specs=[anywhere] * 2,
        out_specs=[VMEM] * 2,
        scratch_shapes=[
            pltpu.VMEM(left.shape, BF16),
            pltpu.VMEM((seqs * count, LANES), F32),
            pltpu.SemaphoreType.DMA((2,)),
        ],
        compiler_params=params(6),
        name="read",
    )(right_hbm, in_hbm(left))
    packed = pl.pallas_call(
        functools.partial(far_kernel, (seqs, width, columns, far_first, far_last)),
        out_shape=[shape(high(u)) for u in far_first * 2] + [shape(high(far_last) // 2)] * 4,
        in_specs=[VMEM],
        out_specs=[VMEM] * (2 * len(far_first) + 4),
        scratch_shapes=[pltpu.VMEM((span, seqs * width), BF16)],
        compiler_params=params(10),
        name="pack_far",
    )(far_right)
    keep = dict(zip(far_first, packed))
    give = dict(zip(far_first, packed[len(far_first) :]))
    singles = packed[2 * len(far_first) :]
    near_pairs = [u for u in near if u[1]]
    packed = pl.pallas_call(
        functools.partial(near_kernel, (seqs, width, columns, near, len(near_pairs))),
        out_shape=[shape(high(u)) for u in near + near_pairs]
        + [jax.ShapeDtypeStruct((pairs, width * width), BF16)],
        in_specs=[anywhere] * 2,
        out_specs=[VMEM] * (len(near + near_pairs) + 1),
        scratch_shapes=[
            pltpu.VMEM((seqs * width, span), BF16),
            pltpu.VMEM((span, seqs * width), BF16),
            pltpu.VMEM(out_weight.shape, BF16),
            pltpu.VMEM((width * width, pairs), F32),
            pltpu.SemaphoreType.DMA((2,)),
        ],
        compiler_params=params(10),
        name="pack_near",
    )(right_hbm, in_hbm(out_weight))
    keep.update(zip(near, packed))
    give.update(zip(near_pairs, packed[len(near) :]))
    turned_weight = packed[-1]

    got = {}

    for units in (far_first, near):
        for unit in units:
            base, step, _ = unit
            value = keep[unit]
            if step:
                theirs = swap(give[unit], 1, n)
                if unit == far_first[0]:
                    got[unit] = [swap(value, base, n, step), swap(theirs, base, n, step)]
                    continue
                value = jnp.concatenate([value, theirs], 0)
            got[unit] = [swap(value, base, n, step) if base else value]
    got[far_last] = []
    for place, value in enumerate(singles):
        distance = far_last[0] + far_last[1] * (place // 2) + place % 2
        got[far_last].append(swap(value, distance, n))
    lefts = left_block
    for distance, step in chain:
        got_left = swap(lefts, distance, n, step)
        lefts = jnp.concatenate([lefts, got_left], 0)
    other_lefts = swap(lefts, 1, n)

    other_core = 1 - lax.rem(lax.axis_index("col"), 2)
    passed = {}
    for units in (near, far_first):
        for unit in units:
            halves = []
            for value in got[unit]:
                parts = value.reshape(-1, 2, high(unit) // 2, LANES)
                half = lax.dynamic_slice_in_dim(parts, other_core, 1, 1)
                halves.append(half.reshape(-1, LANES))
            half = jnp.concatenate(halves, 0) if len(halves) > 1 else halves[0]
            passed[unit] = swap(half, 1, n)

    units = far_first + near
    counts = [len(got[u]) for u in units]
    total, turned_left = pl.pallas_call(
        functools.partial(first_kernel, (seqs, columns, width, units, counts, offsets, first)),
        out_shape=[
            jax.ShapeDtypeStruct((count // 2, pairs, 2 * LANES), F32),
            jax.ShapeDtypeStruct((count * width, cells), BF16),
        ],
        in_specs=[VMEM] * (sum(counts) + len(units) + 3),
        out_specs=[VMEM] * 2,
        scratch_shapes=[pltpu.VMEM((cells, len(first) * per * LANES), BF16)],
        compiler_params=params(24),
        name="first",
    )(*[v for u in units for v in got[u]], *[passed[u] for u in units], lefts, other_lefts, turned_weight)
    units = far_whole + [far_last] + near
    held = [passed[u] for u in units if u in passed]
    counts = [len(got[u]) for u in units]
    return pl.pallas_call(
        functools.partial(last_kernel, (seqs, columns, width, units, counts, offsets, last)),
        out_shape=jax.ShapeDtypeStruct((count, columns, pairs), BF16),
        in_specs=[VMEM] * (sum(counts) + len(held) + 4),
        out_specs=pl.BlockSpec(memory_space=pl.ANY),
        scratch_shapes=[
            pltpu.VMEM((cells, len(last) * per * LANES), BF16),
            pltpu.VMEM((count, columns, pairs), BF16),
            pltpu.SemaphoreType.DMA((count // 2,)),
        ],
        compiler_params=params(24),
        name="last",
    )(
        *[v for u in units for v in got[u]],
        *held,
        turned_left,
        turned_weight,
        total,
        out_bias.reshape(1, pairs),
    )


def solution(mesh):
    n = mesh.shape["col"]

    def on_device(left, right, out_weight, out_bias):
        if fits(left, right, out_weight, n):
            return fast(n, left, right, out_weight, out_bias)
        return general(left, right, out_weight, out_bias)

    in_specs = (P("col", "groups", None), P("col", "groups", None), P(), P())
    out_specs = P("groups", "col", None)
    return jax.shard_map(
        on_device, mesh=mesh, in_specs=in_specs, out_specs=out_specs, check_vma=False
    )
```

```python
import functools

import jax
import jax.numpy as jnp
from jax import lax
from jax.experimental import pallas as pl
from jax.experimental.pallas import tpu as pltpu
from jax.sharding import PartitionSpec as P


LANES = 128
FIRST = 2
ROWS = 512
BF16 = jnp.bfloat16
F32 = jnp.float32
VMEM = pl.BlockSpec(memory_space=pltpu.VMEM)


def tile_update(left_rows, right_cols, out_weight, out_bias):
    seqs, count, width = left_rows.shape
    columns = right_cols.shape[1]
    outer = (
        jnp.einsum("sic,sje->ijce", left_rows, right_cols, preferred_element_type=F32) / seqs
    )
    flat = outer.astype(BF16).reshape(count * columns, width * width)
    update = jnp.dot(flat, out_weight, preferred_element_type=F32) + out_bias
    return update.astype(BF16).reshape(count, columns, out_weight.shape[1])


def rows_update(left_rows, right_cols, out_weight, out_bias):
    seqs, count, width = left_rows.shape
    blocks = jnp.transpose(left_rows.reshape(seqs, count // 8, 8, width), (1, 0, 2, 3))
    results = lax.map(lambda block: tile_update(block, right_cols, out_weight, out_bias), blocks)
    return results.reshape(count, right_cols.shape[1], out_weight.shape[1])


def general(left, right, out_weight, out_bias):
    left_part, right_cols = (
        lax.all_to_all(left, "col", split_axis=1, concat_axis=0, tiled=True),
        lax.all_to_all(right, "col", split_axis=1, concat_axis=0, tiled=True),
    )
    return rows_update(
        lax.all_gather(left_part, "col", axis=1, tiled=True), right_cols, out_weight, out_bias
    )


def turned_order(seqs, width):
    size = seqs * width
    row = lax.broadcasted_iota(jnp.int32, (size, size), 0)
    col = lax.broadcasted_iota(jnp.int32, (size, size), 1)
    return (col == lax.rem(row, seqs) * width + lax.div(row, seqs)).astype(F32).astype(BF16)


def half_start(span, columns, flip):
    upper = lax.div(lax.div(lax.axis_index("col"), 2) * (2 * columns), span)
    return pl.multiple_of((1 - upper if flip else upper) * span, LANES)


def pieces(total):
    return [(begin, min(2 * LANES, total - begin)) for begin in range(0, total, 2 * LANES)]


def turn(source, turned, order, begin, step):
    block = jnp.dot(order, source[:, begin : begin + step], preferred_element_type=F32)
    turned[begin : begin + step, :] = block.astype(BF16).T


def put_core(out_ref, at, turned, offset, start, core, tiles, columns):
    chip = lax.div(lax.axis_index("col"), 2)
    base = jnp.bitwise_xor(chip, lax.div(offset, 2)) * (2 * columns) - start
    rows = pl.ds(pl.multiple_of(base + core * columns, 16), columns)
    for place, tile in enumerate(tiles):
        target = at + place * columns
        out_ref[target : target + columns, :] = turned[rows, tile * LANES : (tile + 1) * LANES]


def put(out_ref, turned, offset, start, tiles, columns):
    for core in range(2):
        at = core * len(tiles) * columns
        put_core(out_ref, at, turned, offset, start, core, tiles, columns)


def put_all(units, turned, start, keep_refs, give_refs, columns):
    core = lax.rem(lax.axis_index("col"), 2)
    for (base, step, tiles), keep, give in zip(units, keep_refs, give_refs):
        put(keep, turned, base + step * core, start, tiles, columns)
        if step:
            put(give, turned, base + step * (1 - core), start, tiles, columns)


def pack_left(left, out_ref, wide):
    seqs, count, width = left.shape
    per = LANES // width
    wide[:, :width] = left[...].astype(F32).reshape(seqs * count, width)
    for group in range(count // per):
        for place in range(per):
            piece = wide[pl.ds(group * per + place, seqs, stride=count), :width]
            out_ref[group * seqs : (group + 1) * seqs, place * width : (place + 1) * width] = (
                piece.astype(BF16)
            )


def read_kernel(columns, right_ref, left_ref, far_out, left_out, left, wide, sems):
    span = far_out.shape[1]
    far = right_ref.at[:, pl.ds(half_start(span, columns, True), span)]
    copies = [
        pltpu.make_async_copy(left_ref, left, sems.at[0]),
        pltpu.make_async_copy(far, far_out, sems.at[1]),
    ]
    for copy in copies:
        copy.start()
    copies[0].wait()
    pack_left(left, left_out, wide)
    copies[1].wait()


def far_kernel(cfg, far_ref, *refs):
    seqs, width, columns, units, (base, step, tiles) = cfg
    keeps, gives = refs[: len(units)], refs[len(units) : 2 * len(units)]
    *singles, turned = refs[2 * len(units) :]
    order = turned_order(seqs, width)
    for begin, size in pieces(turned.shape[0]):
        turn(far_ref, turned, order, begin, size)
    start = half_start(turned.shape[0], columns, True)
    put_all(units, turned, start, keeps, gives, columns)
    core = lax.rem(lax.axis_index("col"), 2)
    for place, ref in enumerate(singles):
        flip, offset = place % 2, base + step * (place // 2)
        put_core(ref, 0, turned, offset, start, jnp.bitwise_xor(core, flip), tiles, columns)


def near_kernel(cfg, right_ref, weight_ref, *refs):
    seqs, width, columns, units, pairs = cfg
    keeps, gives = refs[: len(units)], refs[len(units) : len(units) + pairs]
    weight_out, near, turned, raw, wide, sems = refs[len(units) + pairs :]
    start = half_start(turned.shape[0], columns, False)
    copies = [
        pltpu.make_async_copy(weight_ref, raw, sems.at[0]),
        pltpu.make_async_copy(right_ref.at[:, pl.ds(start, near.shape[1])], near, sems.at[1]),
    ]
    for copy in copies:
        copy.start()
    order = turned_order(seqs, width)
    copies[0].wait()
    wide[...] = raw[...].astype(F32)
    rows = [wide[pl.ds(e, width, stride=width), :] for e in range(width)]
    weight_out[...] = jnp.concatenate(rows, 0).T.astype(BF16)
    copies[1].wait()
    for begin, step in pieces(turned.shape[0]):
        turn(near, turned, order, begin, step)
    given = iter(gives)
    places = [next(given) if step else None for _, step, _ in units]
    put_all(units, turned, start, keeps, places, columns)


def unpack(block, filled, position, place, seqs, columns):
    padded = jnp.concatenate([block, jnp.zeros((LANES - columns, LANES), BF16)], 0).T
    per = LANES // seqs
    rows = pl.ds(pl.multiple_of(position * seqs, 16), seqs)
    for e in range(per):
        lanes = slice((place * per + e) * LANES, (place * per + e + 1) * LANES)
        filled[rows, lanes] = padded[e * seqs : (e + 1) * seqs, :]


def fill(units, tiles, offsets, mine, other, filled, seqs, columns):
    half = len(offsets[0])
    core = lax.rem(lax.axis_index("col"), 2)

    def at(swapped, distance, step=0):
        ends = (distance, distance + step) if step >= 0 else (distance - step, distance)
        first, second = (1, 0) if swapped else (0, 1)
        place = jnp.where(
            core == 0, offsets[first].index(ends[0]), offsets[second].index(ends[1])
        )
        return place + half if swapped else place

    other = iter(other)
    for (base, step, held), own in zip(units, mine):
        passed = None if len(own) == 4 else next(other)
        high = len(held) * columns
        two = 2 * high if len(own) == 1 else 0
        direct = len(own) == 4
        for place, tile in enumerate(tiles):
            inside = held.index(tile) * columns
            if direct:
                blocks = [
                    (ref, inside, at(bool(k % 2), base + step * (k // 2)))
                    for k, ref in enumerate(own)
                ]
            elif step:
                blocks = [
                    (own[0], core * high + inside, at(False, base, step)),
                    (own[-1], two + core * high + inside, at(True, base, step)),
                    (passed, inside, at(True, base, -step)),
                    (passed, high + inside, at(False, base, -step)),
                ]
            else:
                blocks = [
                    (own[0], core * high + inside, at(False, base)),
                    (passed, inside, at(True, base)),
                ]
            for ref, start, position in blocks:
                block = ref[pl.ds(pl.multiple_of(start, 16), columns), :]
                unpack(block, filled, position, place, seqs, columns)


def by_unit(refs, counts):
    mine = []
    for count in counts:
        mine.append(refs[:count])
        refs = refs[count:]
    passed = sum(count < 4 for count in counts)
    return mine, refs[:passed], refs[passed:]


def products(left_ref, weight_ref, filled, tiles, width, per, finish):
    rows = ROWS if left_ref.shape[0] % ROWS == 0 else 256
    group = rows // width
    steps = left_ref.shape[0] // rows
    spots = [(step, place) for step in range(steps) for place in range(len(tiles))]

    def outer_of(step, place):
        block = left_ref[step * rows : (step + 1) * rows, :]
        lanes = slice(place * per * LANES, (place + 1) * per * LANES)
        return jnp.dot(block, filled[:, lanes], preferred_element_type=F32).astype(BF16)

    ahead = outer_of(*spots[0])
    totals = [None] * (group // 2)
    for at, (step, place) in enumerate(spots):
        outer = ahead
        if at + 1 < len(spots):
            ahead = outer_of(*spots[at + 1])
        tile = tiles[place]
        weight = weight_ref[:, tile * per * width : (tile + 1) * per * width]
        for pair in range(group // 2):
            flat = jnp.concatenate(
                [
                    jnp.concatenate(
                        [
                            outer[i * width : (i + 1) * width, e * LANES : (e + 1) * LANES]
                            for e in range(per)
                        ],
                        0,
                    )
                    for i in (2 * pair, 2 * pair + 1)
                ],
                1,
            )
            part = jnp.dot(weight, flat, preferred_element_type=F32)
            totals[pair] = part if place == 0 else totals[pair] + part
        if place == len(tiles) - 1:
            for pair in range(group // 2):
                finish(step * (group // 2) + pair, totals[pair])


def first_kernel(cfg, *refs):
    seqs, columns, width, units, counts, offsets, tiles = cfg
    mine, other, refs = by_unit(refs, counts)
    left_mine, left_other, weight_ref, total_ref, turned_ref, filled = refs
    groups = turned_ref.shape[0] // LANES
    size = groups * seqs
    for group in range(groups):
        rows = [
            ref[place * size + group * seqs : place * size + (group + 1) * seqs, :]
            for ref in (left_mine, left_other)
            for place in range(len(offsets[0]))
        ]
        turned_ref[group * LANES : (group + 1) * LANES, :] = jnp.concatenate(rows, 0).T
    fill(units, tiles, offsets, mine, other, filled, seqs, columns)

    def finish(index, value):
        total_ref[index] = value

    products(turned_ref, weight_ref, filled, tiles, width, LANES // seqs, finish)


def last_kernel(cfg, *refs):
    seqs, columns, width, units, counts, offsets, tiles = cfg
    mine, other, refs = by_unit(refs, counts)
    turned_ref, weight_ref, total_ref, bias_ref, out_ref, filled, ready, sems = refs
    fill(units, tiles, offsets, mine, other, filled, seqs, columns)
    scale = 1.0 / (2 * len(offsets[0]) * seqs)

    def write(index):
        at = pl.ds(2 * index, 2)
        return pltpu.make_async_copy(ready.at[at], out_ref.at[at], sems.at[index])

    def finish(index, value):
        value = (value + total_ref[index]) * scale
        for place in range(2):
            rows = value[:, place * LANES : (place + 1) * LANES].T[:columns, :]
            ready[2 * index + place] = (rows + bias_ref[...]).astype(BF16)
        write(index).start()

    products(turned_ref, weight_ref, filled, tiles, width, LANES // seqs, finish)
    for index in range(sems.shape[0]):
        write(index).wait()


def fits(left, right, out_weight, n):
    seqs, count, width = left.shape
    columns = right.shape[1] // n
    return (
        n >= 8
        and n & (n - 1) == 0
        and n * seqs == 256
        and width == 32
        and seqs == 16
        and columns % 16 == 0
        and columns <= LANES
        and right.shape[1] % (2 * LANES) == 0
        and count % 8 == 0
        and out_weight.shape[1] == LANES
    )


def swap(value, distance, n, by_core=0):
    return lax.ppermute(value, "col", [(i, i ^ (distance + by_core * (i & 1))) for i in range(n)])


def fast(n, left, right, out_weight, out_bias):
    seqs, count, width = left.shape
    columns = right.shape[1] // n
    pairs = out_weight.shape[1]
    per = LANES // seqs
    cells = n * seqs
    span = right.shape[1] // 2
    tiles = tuple(range(width // per))
    first, last = tiles[:FIRST], tiles[FIRST:]
    offsets = ([0], [0])
    chain = []
    distance = n // 2
    while distance > 1:
        step = n // 4 if distance == n // 2 else 0
        chain.append((distance, step))
        offsets = tuple(
            have + [o ^ (distance + step * core) for o in have]
            for core, have in enumerate(offsets)
        )
        distance //= 2
    far = [b for b in range(n // 2, n, 2) if not b & (n // 4)]
    near = [(b, 2, tiles) for b in range(4, n // 2, 4)]
    near += [(2, 0, tiles), (0, 0, tiles)]
    far_whole = [(b, n // 4, tiles) for b in far[:-1]]
    far_first = far_whole + [(far[-1], n // 4, first)]
    far_last = (far[-1], n // 4, last)
    shape = lambda rows: jax.ShapeDtypeStruct((rows, LANES), BF16)
    high = lambda unit: 2 * len(unit[2]) * columns
    in_hbm = lambda x: pltpu.with_memory_space_constraint(x, pltpu.MemorySpace.HBM)
    params = lambda mib: pltpu.CompilerParams(vmem_limit_bytes=mib << 20)
    flat_right = jnp.transpose(right, (0, 2, 1)).reshape(seqs * width, right.shape[1])
    anywhere = pl.BlockSpec(memory_space=pl.ANY)
    right_hbm = in_hbm(flat_right)
    far_right, left_block = pl.pallas_call(
        functools.partial(read_kernel, columns),
        out_shape=[
            jax.ShapeDtypeStruct((seqs * width, span), BF16),
            shape(count * width // LANES * seqs),
        ],
        in_specs=[anywhere] * 2,
        out_specs=[VMEM] * 2,
        scratch_shapes=[
            pltpu.VMEM(left.shape, BF16),
            pltpu.VMEM((seqs * count, LANES), F32),
            pltpu.SemaphoreType.DMA((2,)),
        ],
        compiler_params=params(6),
        name="read",
    )(right_hbm, in_hbm(left))
    packed = pl.pallas_call(
        functools.partial(far_kernel, (seqs, width, columns, far_first, far_last)),
        out_shape=[shape(high(u)) for u in far_first * 2] + [shape(high(far_last) // 2)] * 4,
        in_specs=[VMEM],
        out_specs=[VMEM] * (2 * len(far_first) + 4),
        scratch_shapes=[pltpu.VMEM((span, seqs * width), BF16)],
        compiler_params=params(10),
        name="pack_far",
    )(far_right)
    keep = dict(zip(far_first, packed))
    give = dict(zip(far_first, packed[len(far_first) :]))
    singles = packed[2 * len(far_first) :]
    near_pairs = [u for u in near if u[1]]
    packed = pl.pallas_call(
        functools.partial(near_kernel, (seqs, width, columns, near, len(near_pairs))),
        out_shape=[shape(high(u)) for u in near + near_pairs]
        + [jax.ShapeDtypeStruct((pairs, width * width), BF16)],
        in_specs=[anywhere] * 2,
        out_specs=[VMEM] * (len(near + near_pairs) + 1),
        scratch_shapes=[
            pltpu.VMEM((seqs * width, span), BF16),
            pltpu.VMEM((span, seqs * width), BF16),
            pltpu.VMEM(out_weight.shape, BF16),
            pltpu.VMEM((width * width, pairs), F32),
            pltpu.SemaphoreType.DMA((2,)),
        ],
        compiler_params=params(10),
        name="pack_near",
    )(right_hbm, in_hbm(out_weight))
    keep.update(zip(near, packed))
    give.update(zip(near_pairs, packed[len(near) :]))
    turned_weight = packed[-1]

    got = {}

    for units in (far_first, near):
        for unit in units:
            base, step, _ = unit
            value = keep[unit]
            if step:
                theirs = swap(give[unit], 1, n)
                if unit == far_first[0]:
                    got[unit] = [swap(value, base, n, step), swap(theirs, base, n, step)]
                    continue
                value = jnp.concatenate([value, theirs], 0)
            got[unit] = [swap(value, base, n, step) if base else value]
    got[far_last] = []
    for place, value in enumerate(singles):
        distance = far_last[0] + far_last[1] * (place // 2) + place % 2
        got[far_last].append(swap(value, distance, n))
    lefts = left_block
    for distance, step in chain:
        got_left = swap(lefts, distance, n, step)
        lefts = jnp.concatenate([lefts, got_left], 0)
    other_lefts = swap(lefts, 1, n)

    other_core = 1 - lax.rem(lax.axis_index("col"), 2)
    passed, waiting = {}, []
    for name, units in (("n", near), ("a", far_first)):
        for unit in units:
            halves = []
            for value in got[unit]:
                parts = value.reshape(-1, 2, high(unit) // 2, LANES)
                half = lax.dynamic_slice_in_dim(parts, other_core, 1, 1)
                halves.append(half.reshape(-1, LANES))
            half = jnp.concatenate(halves, 0) if len(halves) > 1 else halves[0]
            if name == "n" and unit[0]:
                waiting.append((unit, half))
            else:
                passed[unit] = swap(half, 1, n)
    at = 0
    joined = swap(jnp.concatenate([half for _, half in waiting], 0), 1, n)
    for unit, half in waiting:
        passed[unit] = joined[at : at + half.shape[0]]
        at += half.shape[0]

    units = far_first + near
    counts = [len(got[u]) for u in units]
    total, turned_left = pl.pallas_call(
        functools.partial(first_kernel, (seqs, columns, width, units, counts, offsets, first)),
        out_shape=[
            jax.ShapeDtypeStruct((count // 2, pairs, 2 * LANES), F32),
            jax.ShapeDtypeStruct((count * width, cells), BF16),
        ],
        in_specs=[VMEM] * (sum(counts) + len(units) + 3),
        out_specs=[VMEM] * 2,
        scratch_shapes=[pltpu.VMEM((cells, len(first) * per * LANES), BF16)],
        compiler_params=params(24),
        name="first",
    )(*[v for u in units for v in got[u]], *[passed[u] for u in units], lefts, other_lefts, turned_weight)
    units = far_whole + [far_last] + near
    held = [passed[u] for u in units if u in passed]
    counts = [len(got[u]) for u in units]
    return pl.pallas_call(
        functools.partial(last_kernel, (seqs, columns, width, units, counts, offsets, last)),
        out_shape=jax.ShapeDtypeStruct((count, columns, pairs), BF16),
        in_specs=[VMEM] * (sum(counts) + len(held) + 4),
        out_specs=pl.BlockSpec(memory_space=pl.ANY),
        scratch_shapes=[
            pltpu.VMEM((cells, len(last) * per * LANES), BF16),
            pltpu.VMEM((count, columns, pairs), BF16),
            pltpu.SemaphoreType.DMA((count // 2,)),
        ],
        compiler_params=params(24),
        name="last",
    )(
        *[v for u in units for v in got[u]],
        *held,
        turned_left,
        turned_weight,
        total,
        out_bias.reshape(1, pairs),
    )


def solution(mesh):
    n = mesh.shape["col"]

    def on_device(left, right, out_weight, out_bias):
        if fits(left, right, out_weight, n):
            return fast(n, left, right, out_weight, out_bias)
        return general(left, right, out_weight, out_bias)

    in_specs = (P("col", "groups", None), P("col", "groups", None), P(), P())
    out_specs = P("groups", "col", None)
    return jax.shard_map(
        on_device, mesh=mesh, in_specs=in_specs, out_specs=out_specs, check_vma=False
    )
```
